32 devices in a mesh: ctx: 8 (over z, core), tp: 4 (over y, x).
Axes of the slice: x: 2, y: 2, z: 4, core: 2. Of those that a mesh axis runs over, the one named last changes fastest.
Arguments:
- hidden_rows: bfloat16 [4096, 8192], P('ctx', 'tp'), may hold values from -6 to 6
- w_value: bfloat16 [8192, 8192], P('ctx', 'tp'), may hold values from -0.0625 to 0.0625
- w_gate: bfloat16 [8192, 8192], P('ctx', 'tp'), may hold values from -0.0625 to 0.0625
- state_proj: bfloat16 [4096, 2, 4, 256], P('ctx'), may hold values from -1.5 to 1.5
- rates: float32 [4096, 128], P('ctx', 'tp'), may hold values from 0 to 4.5, as said below
- read_weights: float32 [6, 4096, 128], P(None, 'ctx', 'tp'), may hold values from 0.25 to 2
- prior_state: float32 [128, 64, 256], P('tp'), may hold values from -24 to 24
- skip_weight: float32 [128], P('tp'), may hold values from 0.5 to 2
- norm_gain: float32 [8192], P('tp'), may hold values from 0.25 to 1.75
Outputs:
- layer_out: bfloat16 [4096, 8192], P('ctx', 'tp')
The draws below stay inside these ranges and needn't reach their ends.
Inputs may be any that keep to these rules, and one draw needn't show every extreme that they name: Positive rates.
All inputs are finite; a program needn't handle non-finite values.
Results may differ from the reference program's by a relative error of at most 0.0085.
Values may be sent and summed in bfloat16 or wider, within the bound.
A program may use at most 128 MiB of HBM per device.

```python
import math
import jax
import jax.numpy as jnp
from jax import lax

D = 8192
HEADS = 128
HEAD_DIM = 64
STATE = 256
HPG = 32
LEVELS = 6
TOK_DEV = 512
TOKENS = 4096
GROUPS = 4


def draw_rates(key, part):
    keys = jax.random.split(key, 7)
    slow_share = 0.5
    is_slow = jax.random.uniform(keys[0], (HEADS,)) < slow_share
    slow_rate = jnp.exp(jax.random.uniform(keys[1], (HEADS,), minval=math.log(0.1 / TOKENS), maxval=math.log(0.6 / TOKENS)))
    fast_rate = jnp.exp(jax.random.uniform(keys[2], (HEADS,), minval=math.log(0.0025), maxval=math.log(0.04)))
    reference_decay_speed = jnp.where(is_slow, slow_rate, fast_rate)
    segment_scaling_factor = jnp.exp(jax.random.uniform(keys[3], (TOKENS // TOK_DEV, HEADS), minval=-0.7, maxval=0.7))
    segment_scaling_factor = jnp.repeat(segment_scaling_factor, TOK_DEV, axis=0)
    stochastic_shift = jax.random.uniform(keys[4], (TOKENS, HEADS), minval=0.5, maxval=2.0)
    spots = jax.random.randint(keys[5], (3,), 0, TOKENS)
    overall_quantity = jax.random.uniform(keys[6], (3, HEADS), minval=0.22, maxval=0.5)
    agreement_tally = (jnp.arange(TOKENS)[:, None] == spots[None, :]).astype(jnp.float32)
    spike_occurrences = jnp.dot(agreement_tally, overall_quantity)
    return (reference_decay_speed[None] * segment_scaling_factor * stochastic_shift + spike_occurrences).astype(jnp.float32)


def block_levels(rng, shape, pieces, low, high):
    level, own = 1.0, jax.random.fold_in(rng, 6)
    for axis_at, parts in pieces:
        steps = jnp.exp(jax.random.uniform(jax.random.fold_in(own, axis_at), (parts,), jnp.float32, low / len(pieces), high / len(pieces)))
        level = level * jnp.repeat(steps, shape[axis_at] // parts).reshape([-1 if axis == axis_at else 1 for axis in range(len(shape))])
    return level


def normal_values(key, dims, scale, most, shards=(), held_as=jnp.bfloat16):
    level = block_levels(key, dims, shards, -0.22, 0.18) if shards else 1.0
    array = jax.random.normal(key, dims, jnp.float32) * scale * level
    return jnp.minimum(jnp.maximum(array, -most), most).astype(held_as)


def setup_inputs(seed: int = 0) -> dict:
    splits = jax.random.split(jax.random.key(seed), 10)
    return {
        "hidden_rows": normal_values(splits[0], (TOKENS, D), 1.0, 6.0, ((0, 8), (1, 4))),
        "w_value": normal_values(splits[1], (D, HEADS * HEAD_DIM), D ** -0.5, 0.0625, ((0, 8), (1, 4))),
        "w_gate": normal_values(splits[2], (D, HEADS * HEAD_DIM), D ** -0.5, 0.0625, ((0, 8), (1, 4))),
        "state_proj": normal_values(splits[3], (TOKENS, 2, GROUPS, STATE), 0.25, 1.5, ((0, 8),)),
        "rates": draw_rates(jax.random.fold_in(splits[9], 71), 0),
        "read_weights": jnp.clip(jnp.exp(math.log(2.0) - 2.0794415 * jax.random.uniform(splits[5], (LEVELS, TOKENS, HEADS), jnp.float32) ** block_levels(splits[5], (LEVELS, TOKENS, HEADS), ((1, 8), (2, 4)), -0.2, 0.2)), 0.25, 2.0),
        "prior_state": normal_values(splits[6], (HEADS, HEAD_DIM, STATE), 4.0, 24.0, ((0, 4),), jnp.float32),
        "skip_weight": jnp.clip(0.5 + 1.5 * jax.random.uniform(splits[7], (HEADS,), jnp.float32) ** block_levels(splits[7], (HEADS,), ((0, 4),), -0.2, 0.2), 0.5, 2.0),
        "norm_gain": jnp.clip(1.0 + 0.15 * jax.random.normal(splits[8], (HEADS * HEAD_DIM,), jnp.float32), 0.25, 1.75),
    }


def level_of(distance, level_count):
    level = jnp.zeros(distance.shape, jnp.int32)
    for bit_pos in range(level_count):
        level = level + (jnp.right_shift(distance, bit_pos) > 0).astype(jnp.int32)
    return level

def reference(hidden_rows, w_value, w_gate, state_proj, rates, read_weights, prior_state, skip_weight, norm_gain):
    spans = TOKENS // TOK_DEV
    values_proj = jnp.dot(hidden_rows, w_value, preferred_element_type=jnp.float32).astype(jnp.bfloat16)
    gates_proj = jnp.dot(hidden_rows, w_gate, preferred_element_type=jnp.float32).astype(jnp.bfloat16)
    writes = state_proj[:, 0].astype(jnp.float32).reshape(spans, TOK_DEV, GROUPS, STATE)
    reads = state_proj[:, 1].astype(jnp.float32).reshape(spans, TOK_DEV, GROUPS, STATE)
    scores = jnp.einsum('ctgn,csgn->gcts', reads, writes)
    level_total = LEVELS - 2
    span_ids = jnp.arange(spans, dtype=jnp.int32)
    levels = level_of(jnp.bitwise_xor(span_ids[:, None], span_ids[None, :]), level_total)
    earlier = span_ids[None, :] < span_ids[:, None]
    onehot = ((levels[:, :, None] == jnp.arange(1, level_total + 1, dtype=jnp.int32)[None, None]) & earlier[:, :, None]).astype(jnp.float32)
    causal = jnp.arange(TOK_DEV)[:, None] >= jnp.arange(TOK_DEV)[None, :]

    def one_head(head_index):
        group_index = head_index // HPG
        rate_head = lax.dynamic_index_in_dim(rates, head_index, 1, keepdims=False).reshape(spans, TOK_DEV)
        cum_rate = jnp.cumsum(rate_head, axis=1)
        values_head = lax.dynamic_slice_in_dim(values_proj, head_index * HEAD_DIM, HEAD_DIM, 1).reshape(spans, TOK_DEV, HEAD_DIM)
        gates_head = lax.dynamic_slice_in_dim(gates_proj, head_index * HEAD_DIM, HEAD_DIM, 1).reshape(spans, TOK_DEV, HEAD_DIM)
        score_head = lax.dynamic_index_in_dim(scores, group_index, 0, keepdims=False)
        write_head = lax.dynamic_index_in_dim(writes, group_index, 2, keepdims=False)
        read_head = lax.dynamic_index_in_dim(reads, group_index, 2, keepdims=False)
        rate_lag = cum_rate[:, :, None] - cum_rate[:, None, :]
        mixing = (jnp.where(causal, jnp.exp(-jnp.where(causal, rate_lag, 0.0)), 0.0) * score_head).astype(jnp.bfloat16)
        local_out = jnp.einsum('cts,csp->ctp', mixing.astype(jnp.float32), values_head.astype(jnp.float32))
        span_total = cum_rate[:, -1]
        write_weighted = (jnp.exp(-(span_total[:, None] - cum_rate))[:, :, None] * write_head).astype(jnp.bfloat16)
        end_state = jnp.einsum('ctn,ctp->cpn', write_weighted.astype(jnp.float32), values_head.astype(jnp.float32))
        before = jnp.cumsum(span_total) - span_total
        exponent = jnp.where(earlier, before[:, None] - before[None, :] - span_total[None, :], 0.0)
        weight = jnp.where(earlier, jnp.exp(-exponent), 0.0)
        coefficient = onehot * weight[:, :, None]
        carried = jnp.einsum('cjl,jpn->clpn', coefficient, end_state, precision=lax.Precision.HIGHEST)
        prior_head = lax.dynamic_index_in_dim(prior_state, head_index, 0, keepdims=False)
        prior_part = jnp.exp(-before)[:, None, None] * prior_head[None]
        states = jnp.concatenate([carried, prior_part[:, None]], axis=1)
        projected = jnp.einsum('ctn,clpn->ctlp', read_head, states, precision=lax.Precision.HIGHEST)
        weights_head = lax.dynamic_index_in_dim(read_weights, head_index, 2, keepdims=False).reshape(LEVELS, spans, TOK_DEV)
        read_scale = jnp.moveaxis(weights_head[1:], 0, 2) * jnp.exp(-cum_rate)[:, :, None]
        carried_out = jnp.einsum('ctl,ctlp->ctp', read_scale, projected, precision=lax.Precision.HIGHEST)
        skip_head = lax.dynamic_index_in_dim(skip_weight, head_index, 0, keepdims=False)
        mixed_out = weights_head[0][:, :, None] * local_out + carried_out + skip_head * values_head.astype(jnp.float32)
        filtered_result = mixed_out * jax.nn.silu(gates_head.astype(jnp.float32))
        inverse = lax.rsqrt(lax.optimization_barrier(jnp.mean(filtered_result * filtered_result, axis=2, keepdims=True)) + 1e-05)
        gain_head = lax.dynamic_slice_in_dim(norm_gain, head_index * HEAD_DIM, HEAD_DIM, 0)
        return (filtered_result * inverse * gain_head).reshape(TOKENS, HEAD_DIM).astype(jnp.bfloat16)
    per_head = lax.map(one_head, jnp.arange(HEADS, dtype=jnp.int32))
    return jnp.transpose(per_head, (1, 0, 2)).reshape(TOKENS, HEADS * HEAD_DIM)
```

```python
import jax
import jax.numpy as jnp
from jax import lax
from jax.sharding import PartitionSpec as P

HEAD_DIM = 64
STATE = 256
HPG = 32
LEVELS = 6


def swapped(value, axis, distance):
    return lax.ppermute(value, axis, [(i, i ^ 1 << distance) for i in range(lax.axis_size(axis))])


def on_device(
    hidden_rows,
    w_value,
    w_gate,
    state_proj,
    rates,
    read_weights,
    prior_state,
    skip_weight,
    norm_gain,
):
    tok_rows = rates.shape[0]
    head_count = rates.shape[1]
    level_total = LEVELS - 2
    ctx_size = lax.axis_size("ctx")
    half = ctx_size // 2
    my_block = lax.axis_index("ctx")
    upper_half = my_block // half
    groups = [list(range(half)), list(range(half, ctx_size))]
    across = [(i, (i + half) % ctx_size) for i in range(ctx_size)]
    w_value_half = lax.all_gather(w_value, "ctx", axis=0, tiled=True, axis_index_groups=groups)
    token_part = lax.all_to_all(hidden_rows, "tp", 0, 1, tiled=True)
    depth = token_part.shape[1] // 2
    kept = lax.dynamic_slice_in_dim(token_part, upper_half * depth, depth, 1)
    given = lax.dynamic_slice_in_dim(token_part, (1 - upper_half) * depth, depth, 1)
    taken = lax.ppermute(given, "ctx", across)
    rows = lax.all_gather(jnp.stack([kept, taken]), "tp", axis=1, tiled=True)
    w_gate_half = lax.all_gather(w_gate, "ctx", axis=0, tiled=True, axis_index_groups=groups)

    def project(weight):
        other = jnp.dot(rows[1], weight, preferred_element_type=jnp.float32).astype(jnp.bfloat16)
        back = lax.ppermute(other, "ctx", across)
        mine = jnp.dot(rows[0], weight, preferred_element_type=jnp.float32)
        return (mine + back.astype(jnp.float32)).astype(jnp.bfloat16)

    values_proj = project(w_value_half)
    gates_proj = project(w_gate_half)
    values3 = values_proj.reshape(tok_rows, head_count, HEAD_DIM)
    group_index = lax.axis_index("tp") * head_count // HPG
    write_vec = lax.dynamic_index_in_dim(state_proj[:, 0], group_index, 1, keepdims=False)
    read_vec = lax.dynamic_index_in_dim(state_proj[:, 1], group_index, 1, keepdims=False)
    cum_rate = jnp.cumsum(rates, axis=0)
    scores = lax.dot_general(
        read_vec, write_vec, (((1,), (1,)), ((), ())), preferred_element_type=jnp.float32
    )
    rate_lag = cum_rate.T[:, :, None] - cum_rate.T[:, None, :]
    causal = (jnp.arange(tok_rows)[:, None] >= jnp.arange(tok_rows)[None, :])[None]
    mixing = (
        jnp.where(causal, jnp.exp(-jnp.where(causal, rate_lag, 0.0)), 0.0) * scores[None]
    ).astype(jnp.bfloat16)
    local_out = jnp.einsum("hts,shp->thp", mixing, values3, preferred_element_type=jnp.float32)
    span_total = cum_rate[-1]
    write_weighted = (
        jnp.exp(-(span_total[None] - cum_rate))[:, :, None]
        * write_vec[:, None, :].astype(jnp.float32)
    ).astype(jnp.bfloat16)
    end_state = jnp.einsum(
        "thn,thp->hpn", write_weighted, values3, preferred_element_type=jnp.float32
    )
    agg_state = end_state
    agg_rate = span_total
    start_rate = jnp.zeros((head_count,), jnp.float32)
    tier_components = []
    bits = ctx_size.bit_length() - 1
    for bit_pos in range(bits):
        is_upper = jnp.right_shift(my_block, bit_pos) % 2 == 1
        if bit_pos < bits - 1:
            other_state, other_rate = swapped((agg_state.astype(jnp.bfloat16), agg_rate), "ctx", bit_pos)
        else:
            share = head_count // half
            piece = lax.dynamic_slice_in_dim(
                agg_state.astype(jnp.bfloat16), (my_block % half) * share, share, 0
            )
            piece, other_rate = swapped((piece, agg_rate), "ctx", bit_pos)
            other_state = lax.all_gather(piece, "ctx", axis=0, tiled=True, axis_index_groups=groups)
        other_state = other_state.astype(jnp.float32)
        tier_components.append(
            jnp.where(is_upper, other_state * jnp.exp(-start_rate)[:, None, None], 0.0).astype(jnp.bfloat16)
        )
        if bit_pos < bits - 1:
            agg_state = jnp.where(
                is_upper,
                other_state * jnp.exp(-agg_rate)[:, None, None] + agg_state,
                agg_state * jnp.exp(-other_rate)[:, None, None] + other_state,
            )
            agg_rate = agg_rate + other_rate
        start_rate = jnp.where(is_upper, start_rate + other_rate, start_rate)
    level_ids = list(range(1, 1 + len(tier_components))) + [level_total + 1]
    prior_part = (jnp.exp(-start_rate)[:, None, None] * prior_state).astype(jnp.bfloat16)
    carried_out = 0.0
    for level, state in zip(level_ids, tier_components + [prior_part]):
        projected = lax.dot_general(
            read_vec, state, (((1,), (2,)), ((), ())), preferred_element_type=jnp.float32
        )
        carried_out = carried_out + read_weights[level][:, :, None] * projected
    carried_out = carried_out * jnp.exp(-cum_rate)[:, :, None]
    mixed_out = (
        read_weights[0][:, :, None] * local_out
        + carried_out
        + skip_weight[None, :, None] * values3.astype(jnp.float32)
    )
    gates3 = gates_proj.reshape(tok_rows, head_count, HEAD_DIM).astype(jnp.float32)
    filtered_result = mixed_out * jax.nn.silu(gates3)
    inverse = lax.rsqrt(jnp.mean(filtered_result * filtered_result, axis=2, keepdims=True) + 1e-05)
    result = filtered_result * inverse * norm_gain.reshape(head_count, HEAD_DIM)[None]
    return result.reshape(tok_rows, head_count * HEAD_DIM).astype(jnp.bfloat16)


def solution(mesh):
    in_specs = (
        P("ctx", "tp"),
        P("ctx", "tp"),
        P("ctx", "tp"),
        P("ctx", None, None, None),
        P("ctx", "tp"),
        P(None, "ctx", "tp"),
        P("tp", None, None),
        P("tp"),
        P("tp"),
    )
    out_specs = P("ctx", "tp")
    return jax.shard_map(
        on_device, mesh=mesh, in_specs=in_specs, out_specs=out_specs, check_vma=False
    )
```

```python
import functools

import jax
import jax.numpy as jnp
from jax import lax
from jax.experimental import pallas as pl
from jax.experimental.pallas import tpu as pltpu

from jax.sharding import PartitionSpec as P

HEAD_DIM = 64
HPG = 32
LEVELS = 6


def swapped(value, axis, distance):
    return lax.ppermute(value, axis, [(i, i ^ 1 << distance) for i in range(lax.axis_size(axis))])


def project_kernel(count, added, place_ref, *refs):
    rows, weights = refs[:count], refs[count : 2 * count]
    total = jnp.dot(rows[0][...], weights[0][...], preferred_element_type=jnp.float32)
    for row, weight in zip(rows[1:], weights[1:]):
        total = total + jnp.dot(row[...], weight[...], preferred_element_type=jnp.float32)
    if added:
        total = total + refs[2 * count][...].astype(jnp.float32)
    refs[-1][...] = total.astype(jnp.bfloat16)


def project(place, rows, blocks, extra=None):
    tok_rows = rows.shape[0]
    depth, width = blocks[0].shape
    tile = min(width, 256)
    masks = range(len(blocks))
    in_specs = [
        pl.BlockSpec((tok_rows, depth), functools.partial(lambda m, i, p: (0, p[0] ^ m), m))
        for m in masks
    ]
    in_specs += [pl.BlockSpec((depth, tile), lambda i, p: (0, i)) for _ in masks]
    operands = [rows] * len(blocks) + list(blocks)
    if extra is not None:
        in_specs.append(pl.BlockSpec((tok_rows, tile), lambda i, p: (0, i)))
        operands.append(extra)
    flops = 2 * tok_rows * depth * len(blocks) * width
    moved = 2 * (rows.size + len(blocks) * depth * width + tok_rows * width)
    return pl.pallas_call(
        functools.partial(project_kernel, len(blocks), extra is not None),
        out_shape=jax.ShapeDtypeStruct((tok_rows, width), jnp.bfloat16),
        grid_spec=pltpu.PrefetchScalarGridSpec(
            num_scalar_prefetch=1,
            grid=(width // tile,),
            in_specs=in_specs,
            out_specs=pl.BlockSpec((tok_rows, tile), lambda i, p: (0, i)),
        ),
        compiler_params=pltpu.CompilerParams(vmem_limit_bytes=40 * 1024 * 1024),
        cost_estimate=pl.CostEstimate(flops=flops, bytes_accessed=moved, transcendentals=0),
    )(place, *operands)


def gather_blocks(weight, half):
    blocks = {0: weight}
    bits = half.bit_length() - 1
    for bit_pos in [*range(1, bits), 0][-bits:] if bits else []:
        for mask in list(blocks):
            blocks[mask | 1 << bit_pos] = swapped(blocks[mask], "ctx", bit_pos)
    return [blocks[mask] for mask in range(half)]


def on_device(
    hidden_rows,
    w_value,
    w_gate,
    state_proj,
    rates,
    read_weights,
    prior_state,
    skip_weight,
    norm_gain,
):
    tok_rows = rates.shape[0]
    head_count = rates.shape[1]
    level_total = LEVELS - 2
    ctx_size = lax.axis_size("ctx")
    half = ctx_size // 2
    my_block = lax.axis_index("ctx")
    upper_half = my_block // half
    groups = [list(range(half)), list(range(half, ctx_size))]
    across = [(i, (i + half) % ctx_size) for i in range(ctx_size)]
    value_blocks = gather_blocks(w_value, half)
    token_part = lax.all_to_all(hidden_rows, "tp", 0, 1, tiled=True)
    depth = token_part.shape[1] // 2
    kept = lax.dynamic_slice_in_dim(token_part, upper_half * depth, depth, 1)
    given = lax.dynamic_slice_in_dim(token_part, (1 - upper_half) * depth, depth, 1)
    taken = lax.ppermute(given, "ctx", across)
    rows_mine = lax.all_gather(kept, "tp", axis=0, tiled=True)
    rows_other = lax.all_gather(taken, "tp", axis=0, tiled=True)
    gate_start, far_block = lax.optimization_barrier((w_gate, value_blocks[half // 2]))
    value_blocks[half // 2] = far_block
    gate_blocks = gather_blocks(gate_start, half)
    place = jnp.reshape(my_block % half, (1,)).astype(jnp.int32)
    value_back = lax.ppermute(project(place, rows_other, value_blocks), "ctx", across)
    gate_other, value_back = lax.optimization_barrier(
        (project(place, rows_other, gate_blocks), value_back)
    )
    gate_back = lax.ppermute(gate_other, "ctx", across)
    values_proj = project(place, rows_mine, value_blocks, value_back)
    gates_proj = project(place, rows_mine, gate_blocks, gate_back)
    values3 = values_proj.reshape(tok_rows, head_count, HEAD_DIM)
    group_index = lax.axis_index("tp") * head_count // HPG
    write_vec = lax.dynamic_index_in_dim(state_proj[:, 0], group_index, 1, keepdims=False)
    read_vec = lax.dynamic_index_in_dim(state_proj[:, 1], group_index, 1, keepdims=False)
    cum_rate = jnp.cumsum(rates, axis=0)
    scores = lax.dot_general(
        read_vec, write_vec, (((1,), (1,)), ((), ())), preferred_element_type=jnp.float32
    )
    rate_lag = cum_rate.T[:, :, None] - cum_rate.T[:, None, :]
    causal = (jnp.arange(tok_rows)[:, None] >= jnp.arange(tok_rows)[None, :])[None]
    mixing = (
        jnp.where(causal, jnp.exp(-jnp.where(causal, rate_lag, 0.0)), 0.0) * scores[None]
    ).astype(jnp.bfloat16)
    local_out = jnp.einsum("hts,shp->thp", mixing, values3, preferred_element_type=jnp.float32)
    span_total = cum_rate[-1]
    write_weighted = (
        jnp.exp(-(span_total[None] - cum_rate))[:, :, None]
        * write_vec[:, None, :].astype(jnp.float32)
    ).astype(jnp.bfloat16)
    end_state = jnp.einsum(
        "thn,thp->hpn", write_weighted, values3, preferred_element_type=jnp.float32
    )
    agg_state = end_state
    agg_rate = span_total
    start_rate = jnp.zeros((head_count,), jnp.float32)
    tier_components = []
    bits = ctx_size.bit_length() - 1
    for bit_pos in range(bits):
        is_upper = jnp.right_shift(my_block, bit_pos) % 2 == 1
        if bit_pos < bits - 1:
            other_state, other_rate = swapped((agg_state.astype(jnp.bfloat16), agg_rate), "ctx", bit_pos)
        else:
            share = head_count // half
            piece = lax.dynamic_slice_in_dim(
                agg_state.astype(jnp.bfloat16), (my_block % half) * share, share, 0
            )
            piece, other_rate = swapped((piece, agg_rate), "ctx", bit_pos)
            other_state = lax.all_gather(piece, "ctx", axis=0, tiled=True, axis_index_groups=groups)
        other_state = other_state.astype(jnp.float32)
        tier_components.append(
            jnp.where(is_upper, other_state * jnp.exp(-start_rate)[:, None, None], 0.0).astype(jnp.bfloat16)
        )
        if bit_pos < bits - 1:
            agg_state = jnp.where(
                is_upper,
                other_state * jnp.exp(-agg_rate)[:, None, None] + agg_state,
                agg_state * jnp.exp(-other_rate)[:, None, None] + other_state,
            )
            agg_rate = agg_rate + other_rate
        start_rate = jnp.where(is_upper, start_rate + other_rate, start_rate)
    level_ids = list(range(1, 1 + len(tier_components))) + [level_total + 1]
    prior_part = (jnp.exp(-start_rate)[:, None, None] * prior_state).astype(jnp.bfloat16)
    carried_out = 0.0
    for level, state in zip(level_ids, tier_components + [prior_part]):
        projected = lax.dot_general(
            read_vec, state, (((1,), (2,)), ((), ())), preferred_element_type=jnp.float32
        )
        carried_out = carried_out + read_weights[level][:, :, None] * projected
    carried_out = carried_out * jnp.exp(-cum_rate)[:, :, None]
    mixed_out = (
        read_weights[0][:, :, None] * local_out
        + carried_out
        + skip_weight[None, :, None] * values3.astype(jnp.float32)
    )
    gates3 = gates_proj.reshape(tok_rows, head_count, HEAD_DIM).astype(jnp.float32)
    filtered_result = mixed_out * jax.nn.silu(gates3)
    inverse = lax.rsqrt(jnp.mean(filtered_result * filtered_result, axis=2, keepdims=True) + 1e-05)
    result = filtered_result * inverse * norm_gain.reshape(head_count, HEAD_DIM)[None]
    return result.reshape(tok_rows, head_count * HEAD_DIM).astype(jnp.bfloat16)


def solution(mesh):
    in_specs = (
        P("ctx", "tp"),
        P("ctx", "tp"),
        P("ctx", "tp"),
        P("ctx", None, None, None),
        P("ctx", "tp"),
        P(None, "ctx", "tp"),
        P("tp", None, None),
        P("tp"),
        P("tp"),
    )
    out_specs = P("ctx", "tp")

    return jax.shard_map(
        on_device, mesh=mesh, in_specs=in_specs, out_specs=out_specs, check_vma=False
    )
```

```python
import functools

import jax
import jax.numpy as jnp
from jax import lax
from jax.experimental import pallas as pl
from jax.experimental.pallas import tpu as pltpu

from jax.sharding import PartitionSpec as P

HEAD_DIM = 64
HPG = 32
LEVELS = 6


def swapped(value, axis, distance):
    return lax.ppermute(value, axis, [(i, i ^ 1 << distance) for i in range(lax.axis_size(axis))])


def project_kernel(count, place_ref, *refs):
    rows, weights = refs[:count], refs[count : 2 * count]
    total = jnp.dot(rows[0][...], weights[0][...], preferred_element_type=jnp.float32)
    for row, weight in zip(rows[1:], weights[1:]):
        total = total + jnp.dot(row[...], weight[...], preferred_element_type=jnp.float32)
    refs[-1][...] = total.astype(refs[-1].dtype)


def project(place, rows, blocks, dtype):
    tok_rows = rows.shape[0]
    depth, width = blocks[0].shape
    tile = min(width, 256)
    masks = range(len(blocks))
    in_specs = [
        pl.BlockSpec((tok_rows, depth), functools.partial(lambda m, i, p: (0, p[0] ^ m), m))
        for m in masks
    ]
    in_specs += [pl.BlockSpec((depth, tile), lambda i, p: (0, i)) for _ in masks]
    operands = [rows] * len(blocks) + list(blocks)
    flops = 2 * tok_rows * depth * len(blocks) * width
    moved = 2 * (rows.size + len(blocks) * depth * width + tok_rows * width)
    return pl.pallas_call(
        functools.partial(project_kernel, len(blocks)),
        out_shape=jax.ShapeDtypeStruct((tok_rows, width), dtype),
        grid_spec=pltpu.PrefetchScalarGridSpec(
            num_scalar_prefetch=1,
            grid=(width // tile,),
            in_specs=in_specs,
            out_specs=pl.BlockSpec((tok_rows, tile), lambda i, p: (0, i)),
        ),
        compiler_params=pltpu.CompilerParams(vmem_limit_bytes=40 * 1024 * 1024),
        cost_estimate=pl.CostEstimate(flops=flops, bytes_accessed=moved, transcendentals=0),
    )(place, *operands)


def gather_blocks(weight, half):
    blocks = {0: weight}
    bits = half.bit_length() - 1
    for bit_pos in [*range(1, bits), 0][-bits:] if bits else []:
        for mask in list(blocks):
            blocks[mask | 1 << bit_pos] = swapped(blocks[mask], "ctx", bit_pos)
    return [blocks[mask] for mask in range(half)]


def on_device(
    hidden_rows,
    w_value,
    w_gate,
    state_proj,
    rates,
    read_weights,
    prior_state,
    skip_weight,
    norm_gain,
):
    tok_rows = rates.shape[0]
    head_count = rates.shape[1]
    level_total = LEVELS - 2
    ctx_size = lax.axis_size("ctx")
    half = ctx_size // 2
    my_block = lax.axis_index("ctx")
    upper_half = my_block // half
    groups = [list(range(half)), list(range(half, ctx_size))]
    across = [(i, (i + half) % ctx_size) for i in range(ctx_size)]
    value_blocks = gather_blocks(w_value, half)
    token_part = lax.all_to_all(hidden_rows, "tp", 0, 1, tiled=True)
    depth = token_part.shape[1] // 2
    kept = lax.dynamic_slice_in_dim(token_part, upper_half * depth, depth, 1)
    given = lax.dynamic_slice_in_dim(token_part, (1 - upper_half) * depth, depth, 1)
    taken = lax.ppermute(given, "ctx", across)
    rows_other = lax.all_gather(taken, "tp", axis=0, tiled=True)
    rows_mine = lax.all_gather(kept, "tp", axis=0, tiled=True)
    gate_start, far_block = lax.optimization_barrier((w_gate, value_blocks[half // 2]))
    value_blocks[half // 2] = far_block
    gate_blocks = gather_blocks(gate_start, half)
    place = jnp.reshape(my_block % half, (1,)).astype(jnp.int32)
    value_other = project(place, rows_other, value_blocks, jnp.bfloat16)
    value_back = lax.ppermute(value_other, "ctx", across)
    value_mine = project(place, rows_mine, value_blocks, jnp.float32)
    gate_other = project(place, rows_other, gate_blocks, jnp.bfloat16)
    gate_back = lax.ppermute(gate_other, "ctx", across)
    gate_mine = project(place, rows_mine, gate_blocks, jnp.float32)
    values_proj = (value_mine + value_back.astype(jnp.float32)).astype(jnp.bfloat16)
    gates_proj = (gate_mine + gate_back.astype(jnp.float32)).astype(jnp.bfloat16)
    values3 = values_proj.reshape(tok_rows, head_count, HEAD_DIM)
    group_index = lax.axis_index("tp") * head_count // HPG
    write_vec = lax.dynamic_index_in_dim(state_proj[:, 0], group_index, 1, keepdims=False)
    read_vec = lax.dynamic_index_in_dim(state_proj[:, 1], group_index, 1, keepdims=False)
    cum_rate = jnp.cumsum(rates, axis=0)
    scores = lax.dot_general(
        read_vec, write_vec, (((1,), (1,)), ((), ())), preferred_element_type=jnp.float32
    )
    rate_lag = cum_rate.T[:, :, None] - cum_rate.T[:, None, :]
    causal = (jnp.arange(tok_rows)[:, None] >= jnp.arange(tok_rows)[None, :])[None]
    mixing = (
        jnp.where(causal, jnp.exp(-jnp.where(causal, rate_lag, 0.0)), 0.0) * scores[None]
    ).astype(jnp.bfloat16)
    local_out = jnp.einsum("hts,shp->thp", mixing, values3, preferred_element_type=jnp.float32)
    span_total = cum_rate[-1]
    write_weighted = (
        jnp.exp(-(span_total[None] - cum_rate))[:, :, None]
        * write_vec[:, None, :].astype(jnp.float32)
    ).astype(jnp.bfloat16)
    end_state = jnp.einsum(
        "thn,thp->hpn", write_weighted, values3, preferred_element_type=jnp.float32
    )
    agg_state = end_state
    agg_rate = span_total
    start_rate = jnp.zeros((head_count,), jnp.float32)
    tier_components = []
    bits = ctx_size.bit_length() - 1
    for bit_pos in range(bits):
        is_upper = jnp.right_shift(my_block, bit_pos) % 2 == 1
        if bit_pos < bits - 1:
            other_state, other_rate = swapped((agg_state.astype(jnp.bfloat16), agg_rate), "ctx", bit_pos)
        else:
            share = head_count // half
            piece = lax.dynamic_slice_in_dim(
                agg_state.astype(jnp.bfloat16), (my_block % half) * share, share, 0
            )
            piece, other_rate = swapped((piece, agg_rate), "ctx", bit_pos)
            other_state = lax.all_gather(piece, "ctx", axis=0, tiled=True, axis_index_groups=groups)
        other_state = other_state.astype(jnp.float32)
        tier_components.append(
            jnp.where(is_upper, other_state * jnp.exp(-start_rate)[:, None, None], 0.0).astype(jnp.bfloat16)
        )
        if bit_pos < bits - 1:
            agg_state = jnp.where(
                is_upper,
                other_state * jnp.exp(-agg_rate)[:, None, None] + agg_state,
                agg_state * jnp.exp(-other_rate)[:, None, None] + other_state,
            )
            agg_rate = agg_rate + other_rate
        start_rate = jnp.where(is_upper, start_rate + other_rate, start_rate)
    level_ids = list(range(1, 1 + len(tier_components))) + [level_total + 1]
    prior_part = (jnp.exp(-start_rate)[:, None, None] * prior_state).astype(jnp.bfloat16)
    carried_out = 0.0
    for level, state in zip(level_ids, tier_components + [prior_part]):
        projected = lax.dot_general(
            read_vec, state, (((1,), (2,)), ((), ())), preferred_element_type=jnp.float32
        )
        carried_out = carried_out + read_weights[level][:, :, None] * projected
    carried_out = carried_out * jnp.exp(-cum_rate)[:, :, None]
    mixed_out = (
        read_weights[0][:, :, None] * local_out
        + carried_out
        + skip_weight[None, :, None] * values3.astype(jnp.float32)
    )
    gates3 = gates_proj.reshape(tok_rows, head_count, HEAD_DIM).astype(jnp.float32)
    filtered_result = mixed_out * jax.nn.silu(gates3)
    inverse = lax.rsqrt(jnp.mean(filtered_result * filtered_result, axis=2, keepdims=True) + 1e-05)
    result = filtered_result * inverse * norm_gain.reshape(head_count, HEAD_DIM)[None]
    return result.reshape(tok_rows, head_count * HEAD_DIM).astype(jnp.bfloat16)


def solution(mesh):
    in_specs = (
        P("ctx", "tp"),
        P("ctx", "tp"),
        P("ctx", "tp"),
        P("ctx", None, None, None),
        P("ctx", "tp"),
        P(None, "ctx", "tp"),
        P("tp", None, None),
        P("tp"),
        P("tp"),
    )
    out_specs = P("ctx", "tp")

    return jax.shard_map(
        on_device, mesh=mesh, in_specs=in_specs, out_specs=out_specs, check_vma=False
    )
```

```python
import functools

import jax
import jax.numpy as jnp
from jax import lax
from jax.experimental import pallas as pl
from jax.experimental.pallas import tpu as pltpu

from jax.sharding import PartitionSpec as P

HEAD_DIM = 64
HPG = 32
LEVELS = 6


def swapped(value, axis, distance):
    return lax.ppermute(value, axis, [(i, i ^ 1 << distance) for i in range(lax.axis_size(axis))])


def project_kernel(count, place_ref, *refs):
    rows, weights = refs[:count], refs[count : 2 * count]
    total = jnp.dot(rows[0][...], weights[0][...], preferred_element_type=jnp.float32)
    for row, weight in zip(rows[1:], weights[1:]):
        total = total + jnp.dot(row[...], weight[...], preferred_element_type=jnp.float32)
    refs[-1][...] = total.astype(refs[-1].dtype)


def project(place, rows, blocks, dtype):
    tok_rows = rows.shape[0]
    depth, width = blocks[0].shape
    tile = min(width, 256)
    masks = range(len(blocks))
    in_specs = [
        pl.BlockSpec((tok_rows, depth), functools.partial(lambda m, i, p: (0, p[0] ^ m), m))
        for m in masks
    ]
    in_specs += [pl.BlockSpec((depth, tile), lambda i, p: (0, i)) for _ in masks]
    operands = [rows] * len(blocks) + list(blocks)
    flops = 2 * tok_rows * depth * len(blocks) * width
    moved = 2 * (rows.size + len(blocks) * depth * width + tok_rows * width)
    return pl.pallas_call(
        functools.partial(project_kernel, len(blocks)),
        out_shape=jax.ShapeDtypeStruct((tok_rows, width), dtype),
        grid_spec=pltpu.PrefetchScalarGridSpec(
            num_scalar_prefetch=1,
            grid=(width // tile,),
            in_specs=in_specs,
            out_specs=pl.BlockSpec((tok_rows, tile), lambda i, p: (0, i)),
        ),
        compiler_params=pltpu.CompilerParams(vmem_limit_bytes=40 * 1024 * 1024),
        cost_estimate=pl.CostEstimate(flops=flops, bytes_accessed=moved, transcendentals=0),
    )(place, *operands)


def gather_blocks(weight, half):
    blocks = {0: weight}
    bits = half.bit_length() - 1
    for bit_pos in [*range(1, bits), 0][-bits:] if bits else []:
        for mask in list(blocks):
            blocks[mask | 1 << bit_pos] = swapped(blocks[mask], "ctx", bit_pos)
    return [blocks[mask] for mask in range(half)]


def on_device(
    hidden_rows,
    w_value,
    w_gate,
    state_proj,
    rates,
    read_weights,
    prior_state,
    skip_weight,
    norm_gain,
):
    tok_rows = rates.shape[0]
    head_count = rates.shape[1]
    level_total = LEVELS - 2
    ctx_size = lax.axis_size("ctx")
    half = ctx_size // 2
    my_block = lax.axis_index("ctx")
    upper_half = my_block // half
    groups = [list(range(half)), list(range(half, ctx_size))]
    across = [(i, (i + half) % ctx_size) for i in range(ctx_size)]
    chunks = 2
    width = w_value.shape[1] // chunks
    moved = {}
    for part, weight in (("value", w_value), ("gate", w_gate)):
        for chunk in range(chunks):
            piece = lax.slice_in_dim(weight, chunk * width, (chunk + 1) * width, axis=1)
            moved[part, chunk] = gather_blocks(piece, half)
    token_part = lax.all_to_all(hidden_rows, "tp", 0, 1, tiled=True)
    depth = token_part.shape[1] // 2
    kept = lax.dynamic_slice_in_dim(token_part, upper_half * depth, depth, 1)
    given = lax.dynamic_slice_in_dim(token_part, (1 - upper_half) * depth, depth, 1)
    taken = lax.ppermute(given, "ctx", across)
    rows_other = lax.all_gather(taken, "tp", axis=0, tiled=True)
    rows_mine = lax.all_gather(kept, "tp", axis=0, tiled=True)
    place = jnp.reshape(my_block % half, (1,)).astype(jnp.int32)
    sums = {}
    for (part, chunk), blocks in moved.items():
        back = lax.ppermute(project(place, rows_other, blocks, jnp.bfloat16), "ctx", across)
        mine = project(place, rows_mine, blocks, jnp.float32)
        sums[part, chunk] = (mine + back.astype(jnp.float32)).astype(jnp.bfloat16)
    values_proj = jnp.concatenate([sums["value", chunk] for chunk in range(chunks)], axis=1)
    gates_proj = jnp.concatenate([sums["gate", chunk] for chunk in range(chunks)], axis=1)
    values3 = values_proj.reshape(tok_rows, head_count, HEAD_DIM)
    group_index = lax.axis_index("tp") * head_count // HPG
    write_vec = lax.dynamic_index_in_dim(state_proj[:, 0], group_index, 1, keepdims=False)
    read_vec = lax.dynamic_index_in_dim(state_proj[:, 1], group_index, 1, keepdims=False)
    cum_rate = jnp.cumsum(rates, axis=0)
    scores = lax.dot_general(
        read_vec, write_vec, (((1,), (1,)), ((), ())), preferred_element_type=jnp.float32
    )
    rate_lag = cum_rate.T[:, :, None] - cum_rate.T[:, None, :]
    causal = (jnp.arange(tok_rows)[:, None] >= jnp.arange(tok_rows)[None, :])[None]
    mixing = (
        jnp.where(causal, jnp.exp(-jnp.where(causal, rate_lag, 0.0)), 0.0) * scores[None]
    ).astype(jnp.bfloat16)
    local_out = jnp.einsum("hts,shp->thp", mixing, values3, preferred_element_type=jnp.float32)
    span_total = cum_rate[-1]
    write_weighted = (
        jnp.exp(-(span_total[None] - cum_rate))[:, :, None]
        * write_vec[:, None, :].astype(jnp.float32)
    ).astype(jnp.bfloat16)
    end_state = jnp.einsum(
        "thn,thp->hpn", write_weighted, values3, preferred_element_type=jnp.float32
    )
    agg_state = end_state
    agg_rate = span_total
    start_rate = jnp.zeros((head_count,), jnp.float32)
    tier_components = []
    bits = ctx_size.bit_length() - 1
    for bit_pos in range(bits):
        is_upper = jnp.right_shift(my_block, bit_pos) % 2 == 1
        if bit_pos < bits - 1:
            other_state, other_rate = swapped((agg_state.astype(jnp.bfloat16), agg_rate), "ctx", bit_pos)
        else:
            share = head_count // half
            piece = lax.dynamic_slice_in_dim(
                agg_state.astype(jnp.bfloat16), (my_block % half) * share, share, 0
            )
            piece, other_rate = swapped((piece, agg_rate), "ctx", bit_pos)
            other_state = lax.all_gather(piece, "ctx", axis=0, tiled=True, axis_index_groups=groups)
        other_state = other_state.astype(jnp.float32)
        tier_components.append(
            jnp.where(is_upper, other_state * jnp.exp(-start_rate)[:, None, None], 0.0).astype(jnp.bfloat16)
        )
        if bit_pos < bits - 1:
            agg_state = jnp.where(
                is_upper,
                other_state * jnp.exp(-agg_rate)[:, None, None] + agg_state,
                agg_state * jnp.exp(-other_rate)[:, None, None] + other_state,
            )
            agg_rate = agg_rate + other_rate
        start_rate = jnp.where(is_upper, start_rate + other_rate, start_rate)
    level_ids = list(range(1, 1 + len(tier_components))) + [level_total + 1]
    prior_part = (jnp.exp(-start_rate)[:, None, None] * prior_state).astype(jnp.bfloat16)
    carried_out = 0.0
    for level, state in zip(level_ids, tier_components + [prior_part]):
        projected = lax.dot_general(
            read_vec, state, (((1,), (2,)), ((), ())), preferred_element_type=jnp.float32
        )
        carried_out = carried_out + read_weights[level][:, :, None] * projected
    carried_out = carried_out * jnp.exp(-cum_rate)[:, :, None]
    mixed_out = (
        read_weights[0][:, :, None] * local_out
        + carried_out
        + skip_weight[None, :, None] * values3.astype(jnp.float32)
    )
    gates3 = gates_proj.reshape(tok_rows, head_count, HEAD_DIM).astype(jnp.float32)
    filtered_result = mixed_out * jax.nn.silu(gates3)
    inverse = lax.rsqrt(jnp.mean(filtered_result * filtered_result, axis=2, keepdims=True) + 1e-05)
    result = filtered_result * inverse * norm_gain.reshape(head_count, HEAD_DIM)[None]
    return result.reshape(tok_rows, head_count * HEAD_DIM).astype(jnp.bfloat16)


def solution(mesh):
    in_specs = (
        P("ctx", "tp"),
        P("ctx", "tp"),
        P("ctx", "tp"),
        P("ctx", None, None, None),
        P("ctx", "tp"),
        P(None, "ctx", "tp"),
        P("tp", None, None),
        P("tp"),
        P("tp"),
    )
    out_specs = P("ctx", "tp")

    return jax.shard_map(
        on_device, mesh=mesh, in_specs=in_specs, out_specs=out_specs, check_vma=False
    )
```
